32 devices in a mesh: tp: 4 (over y, x), row: 4 (over z), col: 2 (over core).
Axes of the slice: x: 2, y: 2, z: 4, core: 2. Of those that a mesh axis runs over, the one named last changes fastest.
Arguments:
- hidden: bfloat16 [128, 14336], P('col', 'row'), may hold values from -6 to 6
- out_grad: bfloat16 [128, 4096], P(None, ('tp', 'row')), may hold values from -6 to 6
- basis_in: bfloat16 [14336, 4096], P(('row', 'col'), 'tp'), may hold values from -0.046875 to 0.046875
- basis_out: bfloat16 [4096, 1024], P(('tp', 'row'), 'col'), may hold values from -0.09375 to 0.09375
- eigen: float32 [4096, 1024], P(('tp', 'row'), 'col'), may hold values from 0.02 to 2
Outputs:
- precond: float32 [4096, 14336], P(('tp', 'col'), 'row')
The draws below stay inside these ranges and needn't reach their ends.
All inputs are finite; a program needn't handle non-finite values.
Results may differ from the reference program's by a relative error of at most 0.024.
Values may be sent and summed in bfloat16 or wider, within the bound.
No kernel may reach another device: no remote copies, remote signals or barrier semaphores. Data moves between devices by JAX's collectives and lax.ppermute only.
A program may use at most 64 MiB of HBM per device.

```python
import math
import jax
import jax.numpy as jnp
from jax import lax

D = 4096
FF = 14336
KIN = 4096
KOUT = 1024
TQ = 128
N_TP = 4
N_COL = 2


def block_scale(rng, shape, shards, smallest, largest):
    level = 1.0
    for dim, shards_of in shards:
        heights = jax.random.uniform(jax.random.fold_in(jax.random.fold_in(rng, 6), dim), (shards_of,), jnp.float32, smallest / len(shards), largest / len(shards))
        level = level * jnp.repeat(jnp.exp(heights), shape[dim] // shards_of).reshape((-1,) + (1,) * (len(shape) - 1 - dim))
    return level


def centred(own_key, extent, scale, bound, pieces=(), held_as=jnp.bfloat16):
    array = jax.random.normal(own_key, extent, jnp.float32) * scale
    if len(pieces) > 0:
        array = block_scale(own_key, extent, pieces, -0.22, 0.18) * array
    return jnp.clip(array, min=-bound, max=bound).astype(held_as)


def setup_inputs(seed: int = 0) -> dict:
    seeds = jax.random.split(jax.random.key(seed), 6)
    hidden = centred(seeds[0], (TQ, FF), 1.0, 6.0, ((0, 2), (1, 4)))
    out_grad = centred(seeds[1], (TQ, D), 1.0, 6.0, ((1, 16),))
    basis_in = centred(seeds[2], (FF, KIN), FF ** -0.5, 0.046875, ((0, 8), (1, 4)))
    basis_out = centred(seeds[3], (D, KOUT), D ** -0.5, 0.09375, ((0, 16), (1, 2)))
    eigen = jnp.clip(jnp.exp(math.log(2.0) - 4.6051702 * jax.random.uniform(seeds[4], (KIN, KOUT), jnp.float32) ** block_scale(seeds[4], (KIN, KOUT), ((0, 16), (1, 2)), -0.2, 0.2)), 0.02, 2.0)
    return {"hidden": hidden, "out_grad": out_grad, "basis_in": basis_in, "basis_out": basis_out, "eigen": eigen}


damping = 0.01


def reference(hidden, out_grad, basis_in, basis_out, eigen):
    rot_in = jnp.dot(hidden, basis_in, preferred_element_type=jnp.float32).astype(jnp.bfloat16)
    rot_out = jnp.dot(out_grad, basis_out, preferred_element_type=jnp.float32).astype(jnp.bfloat16)
    coeff = jnp.dot(rot_out.T, rot_in, preferred_element_type=jnp.float32)
    scaled = (coeff / (TQ * (eigen.T + damping))).astype(jnp.bfloat16)
    out_block = KOUT // N_COL
    mixed = jnp.zeros((D, KIN), jnp.float32)
    for index in range(N_COL):
        part = jnp.dot(basis_out[:, index * out_block:(index + 1) * out_block], scaled[index * out_block:(index + 1) * out_block], preferred_element_type=jnp.float32)
        part = lax.optimization_barrier(part.astype(jnp.bfloat16))
        mixed = mixed + part.astype(jnp.float32)
    mixed = mixed.astype(jnp.bfloat16)
    in_block = KIN // N_TP
    result = jnp.zeros((D, FF), jnp.float32)
    for index in range(N_TP):
        part = jnp.dot(mixed[:, index * in_block:(index + 1) * in_block], basis_in[:, index * in_block:(index + 1) * in_block].T, preferred_element_type=jnp.float32)
        part = lax.optimization_barrier(part.astype(jnp.bfloat16))
        result = result + part.astype(jnp.float32)
    return result
```

```python
import jax
import jax.numpy as jnp
from jax import lax
from jax.sharding import PartitionSpec as P

damping = 0.01
chunks_per_part = 2


def contract(left, right, dims):
    return lax.dot_general(left, right, (dims, ((), ())), preferred_element_type=jnp.float32)


def low(array):
    return array.astype(jnp.bfloat16)


def wide(array):
    return array.astype(jnp.float32)


def shift(array, axis, by):
    count = lax.axis_size(axis)
    return lax.ppermute(array, axis, [(i, (i + by) % count) for i in range(count)])


def flip(array, axis, bit):
    count = lax.axis_size(axis)
    return lax.ppermute(array, axis, [(i, i ^ bit) for i in range(count)])


def block(array, dim, index, size):
    return lax.dynamic_slice_in_dim(array, index * size, size, dim)


def gather(array, axis, dim):
    count = lax.axis_size(axis)
    index = lax.axis_index(axis)
    size = array.shape[dim]
    shape = list(array.shape)
    shape[dim] = size * count
    whole = jnp.zeros(shape, array.dtype)
    for by in range(count):
        piece = array if by == 0 else shift(array, axis, by)
        source = (index - by + count) % count
        whole = lax.dynamic_update_slice_in_dim(whole, piece, source * size, dim)
    return whole


def scatter(array, axis, dim):
    count = lax.axis_size(axis)
    index = lax.axis_index(axis)
    size = array.shape[dim] // count
    array = low(array)
    total = wide(block(array, dim, index, size))
    for by in range(1, count):
        total = total + wide(shift(block(array, dim, (index + by) % count, size), axis, by))
    return total


def split(total, pieces):
    unit = 1
    for trial in (128, 16, 8):
        if total % trial == 0 and total // trial >= pieces:
            unit = trial
            break
    units = total // unit
    sizes = [unit * (units // pieces + (1 if i < units % pieces else 0)) for i in range(pieces)]
    return [size for size in sizes if size > 0]


def shards(hidden, out_grad, basis_in, basis_out, eigen):
    tp_count = lax.axis_size("tp")
    col_count = lax.axis_size("col")
    tp_index = lax.axis_index("tp")
    col_index = lax.axis_index("col")
    bits = [1 << i for i in range(tp_count.bit_length() - 1)]
    queries = out_grad.shape[0]
    units = basis_in.shape[0]

    partial_out = contract(out_grad, basis_out, ((1,), (0,)))
    rotated_out = scatter(partial_out, "row", 0)
    for bit in bits:
        rotated_out = rotated_out + wide(flip(low(rotated_out), "tp", bit))
    rotated_out = gather(low(rotated_out), "row", 0)
    rotated_out = gather(rotated_out, "col", 1)

    own = None
    for by in range(col_count):
        peer = (col_index + by) % col_count
        part = block(hidden, 1, peer, units)
        if by == 0:
            own = contract(part, basis_in, ((1,), (0,)))
            continue
        part = shift(part, "col", by)
        product = low(contract(part, basis_in, ((1,), (0,))))
        own = own + wide(shift(product, "col", col_count - by))
    rotated_in = scatter(own, "row", 1)
    rotated_in = gather(low(rotated_in), "row", 1)
    rotated_in = gather(rotated_in, "col", 0)

    scale = low(1.0 / (queries * (eigen + damping)))
    scale = gather(gather(scale, "row", 0), "col", 1)

    outputs = gather(gather(basis_out, "row", 0), "col", 1)

    directions = scale.shape[1] // tp_count

    def relative(array):
        return [block(array, 1, tp_index ^ j, directions) for j in range(tp_count)]

    scaled = []
    for turned, factor in zip(relative(rotated_out), relative(scale)):
        coeff = contract(rotated_in, turned, ((0,), (0,)))
        scaled.append(low(coeff * wide(factor)))
    outputs = jnp.concatenate(relative(outputs), axis=1)

    out_rows = outputs.shape[0] // col_count
    result = jnp.zeros((out_rows, units * col_count), jnp.float32)

    start = 0
    parts = split(units, len(bits) * chunks_per_part)
    for number, rows in enumerate(parts):
        turn = number % len(bits)
        order = bits[turn:] + bits[:turn]
        hidden_rows = basis_in[start:start + rows]
        keys = list(range(tp_count))
        held = {}
        received = {}
        for stage, bit in enumerate(order):
            sending = [j for j in keys if j & bit]
            keys = [j for j in keys if not j & bit]
            if stage == 0:
                weights = jnp.concatenate([scaled[j] for j in sending], axis=1)
                packet = low(contract(hidden_rows, weights, ((1,), (0,))))
                for j in keys:
                    held[j] = contract(hidden_rows, scaled[j], ((1,), (0,)))
            else:
                packet = low(jnp.concatenate([held[j] for j in sending], axis=1))
            packet = flip(packet, "tp", bit)
            for place, j in enumerate(sending):
                piece = packet[:, place * directions:(place + 1) * directions]
                held[j ^ bit] = held[j ^ bit] + wide(piece)
        found = [low(held[0])]
        names = [0]
        for bit in reversed(order):
            packet = found[0] if len(found) == 1 else jnp.concatenate(found, axis=1)
            found = [packet, flip(packet, "tp", bit)]
            names = names + [j ^ bit for j in names]
            found = [jnp.concatenate(found, axis=1)]
        mixed = found[0]
        basis = jnp.concatenate(
            [outputs[:, j * directions:(j + 1) * directions] for j in names], axis=1
        )
        for by in range(col_count):
            peer = (col_index + by) % col_count
            product = contract(block(basis, 0, peer, out_rows), mixed, ((1,), (1,)))
            source = col_index
            if by > 0:
                product = wide(shift(low(product), "col", by))
                source = (col_index - by + col_count) % col_count
            result = lax.dynamic_update_slice(result, product, (0, source * units + start))
        start += rows
    return result


def solution(mesh):
    placed = (
        P("col", "row"),
        P(None, ("tp", "row")),
        P(("row", "col"), "tp"),
        P(("tp", "row"), "col"),
        P(("tp", "row"), "col"),
    )
    return jax.shard_map(
        shards, mesh=mesh, in_specs=placed, out_specs=P(("tp", "col"), "row"), check_vma=False
    )
```
